1024 devices in a mesh: hb: 16 (over x, core), wb: 8 (over y), hd: 8 (over z).
Axes of the slice: x: 8, y: 8, z: 8, core: 2. Of those that a mesh axis runs over, the one named last changes fastest.
Arguments:
- query_rows: bfloat16 [24, 16, 16, 64, 128], P('hd', 'hb', 'wb'), may hold values from -180 to 180
- key_rows: bfloat16 [24, 16, 16, 64, 128], P('hd', 'hb', 'wb'), may hold values from -6 to 6
- value_rows: bfloat16 [24, 16, 16, 64, 128], P('hd', 'hb', 'wb'), may hold values from -6 to 6
- grad_out: bfloat16 [24, 16, 16, 64, 128], P('hd', 'hb', 'wb'), may hold values from -6 to 6
- sel_tiles: int32 [16, 16, 8], P(None, 'wb'), may hold values from 0 to 31
- sel_count: int32 [16, 16], P(None, 'wb'), may hold values from 1 to 8, as said below
- tile_radius: int32 [24], P('hd'), may hold values from 0 to 1
Outputs:
- grad_query: bfloat16 [24, 16, 16, 64, 128], P('hd', 'hb', 'wb')
- grad_key: bfloat16 [24, 16, 16, 64, 128], P('hd', 'hb', 'wb')
- grad_value: bfloat16 [24, 16, 16, 64, 128], P('hd', 'hb', 'wb')
The draws below stay inside these ranges and needn't reach their ends.
Inputs may be any that keep to these rules, and one draw needn't show every extreme that they name: sel_count[r, c] is the number of live entries of that query tile's list, from 1 to 8; entries of sel_tiles at positions sel_count or beyond are ignored, and entries may repeat.
All inputs are finite; a program needn't handle non-finite values.
Results may differ from the reference program's by a relative error of at most 0.022.
Values may be sent and summed in bfloat16 or wider, within the bound.
No kernel may reach another device: no remote copies, remote signals or barrier semaphores. Data moves between devices by JAX's collectives and lax.ppermute only.
A program may use at most 64 MiB of HBM per device.

```python
import jax
import jax.numpy as jnp
from jax import lax

HD = 128
TILE = 64
SEL = 8
TR = 1
TC = 2
HEADS = 24
GR = 16
GC = 16
N_HB = 16
N_WB = 8


def key_base(key):
    shape = (HEADS, GR, GC, TILE, HD)
    return jax.random.truncated_normal(jax.random.fold_in(key, 7), -6.0, 6.0, shape, jnp.float32)


def draw_key_rows(key, part):
    base = key_base(key)
    return base.astype(jnp.bfloat16)


def draw_query_rows(key, part):
    shape = (HEADS, GR, GC, TILE, HD)
    fresh = jax.random.truncated_normal(jax.random.fold_in(key, 13), -6.0, 6.0, shape, jnp.float32)
    return fresh.astype(jnp.bfloat16)


def draw_sel_count(key, part):
    level = jax.random.randint(jax.random.fold_in(key, 29), (GR, 1), 1, 5)
    base = jax.random.randint(jax.random.fold_in(key, 31), (GR, GC), 0, SEL)
    counted = 1 + base * level // 4
    pick_row = jax.random.randint(jax.random.fold_in(key, 37), (), 0, GR)
    pick_col = jax.random.randint(jax.random.fold_in(key, 41), (), 0, GC)
    marked = (jnp.arange(GR)[:, None] == pick_row) & (jnp.arange(GC)[None, :] == pick_col)
    return jnp.where(marked, SEL, counted).astype(jnp.int32)


def draw_tile_radius(key, part):
    picked = jax.random.randint(jax.random.fold_in(key, 23), (HEADS,), 0, 2)
    order = jax.random.permutation(jax.random.fold_in(key, 43), HEADS)
    picked = picked.at[order[0]].set(0)
    picked = picked.at[order[1]].set(1)
    return picked.astype(jnp.int32)


def touch_ends(entries, own_key, smallest, top_value):
    index_at = [jax.random.randint(jax.random.fold_in(own_key, axis), (), 0, length) for axis, length in enumerate(entries.shape)]
    widest = entries.shape.index(max(entries.shape))
    beside = index_at[:widest] + [(index_at[widest] + 1) % entries.shape[widest]] + index_at[widest + 1:]
    return entries.at[tuple(index_at)].set(smallest).at[tuple(beside)].set(top_value)


def levels(own_key, extent, pieces, low, top_value):
    gain = 1.0
    for axis_at, shards_of in pieces:
        steps = jax.random.uniform(jax.random.fold_in(jax.random.fold_in(own_key, 6), axis_at), (shards_of,), jnp.float32, low / len(pieces), top_value / len(pieces))
        gain = gain * jnp.repeat(jnp.exp(steps), extent[axis_at] // shards_of).reshape((-1,) + (1,) * (len(extent) - 1 - axis_at))
    return gain


def normal_values(key, dims, scale, bound, pieces=(), kind=jnp.bfloat16):
    entries = scale * jax.random.normal(key, dims, jnp.float32)
    if pieces:
        entries = entries * levels(key, dims, pieces, -0.22, 0.18)
    return jnp.clip(entries, -bound, bound).astype(kind)


def setup_inputs(seed: int = 0) -> dict:
    key_list = jax.random.split(jax.random.key(seed), 8)
    return {
        "query_rows": draw_query_rows(jax.random.fold_in(key_list[7], 71), 0),
        "key_rows": draw_key_rows(jax.random.fold_in(key_list[7], 71), 0),
        "value_rows": normal_values(key_list[2], (HEADS, GR, GC, TILE, HD), 1.0, 6.0, ((0, 8), (1, 16), (2, 8))),
        "grad_out": normal_values(key_list[3], (HEADS, GR, GC, TILE, HD), 1.0, 6.0, ((0, 8), (1, 16), (2, 8))),
        "sel_tiles": touch_ends(jax.random.randint(key_list[4], (GR, GC, SEL), 0, GR * TC), jax.random.fold_in(key_list[4], 1), 0, (GR * TC) - 1).astype(jnp.int32),
        "sel_count": draw_sel_count(jax.random.fold_in(key_list[7], 71), 0),
        "tile_radius": draw_tile_radius(jax.random.fold_in(key_list[7], 71), 0),
    }


def settle(values):
    return lax.optimization_barrier(values.astype(jnp.bfloat16)).astype(jnp.float32)


def tile_masks(tile_radius, sel_tiles, sel_count):
    band_rows, band_cols, picks = sel_tiles.shape
    tile_total = band_rows * band_cols
    tile_index = jnp.arange(tile_total, dtype=jnp.int32)
    row_of = tile_index // band_cols
    col_of = tile_index % band_cols
    spread = jnp.abs(row_of[:, None] - row_of[None, :]) + jnp.abs(col_of[:, None] - col_of[None, :])
    nearby = spread[None] <= tile_radius[:, None, None]
    live_pick = jnp.arange(picks, dtype=jnp.int32)[None, :] < sel_count.reshape(tile_total, 1)
    matches = (sel_tiles.reshape(tile_total, picks, 1) == tile_index[None, None, :]) & live_pick[:, :, None]
    return nearby | jnp.any(matches, axis=1)[None]


def to_band(values):
    extra = values.shape[3:]
    moved = jnp.moveaxis(values.reshape((GR, N_WB, TC, TILE) + extra), 1, 0)
    return moved.reshape((N_WB, GR * TC * TILE) + extra)


def to_grid(values):
    extra = values.shape[2:]
    moved = jnp.moveaxis(values.reshape((N_WB, GR, TC, TILE) + extra), 0, 1)
    return moved.reshape((GR, GC, TILE) + extra)


def head_grads(query, keyrow, valrow, cotan, radius, allowed):
    factor = HD ** -0.5
    f32 = jnp.float32
    query_f = query.astype(f32)
    key_f = keyrow.astype(f32)
    value_f = valrow.astype(f32)
    cotan_f = cotan.astype(f32)
    band_q = to_band(query_f)
    band_k = to_band(key_f)
    band_v = to_band(value_f)
    band_d = to_band(cotan_f)
    tile_total = GR * TC
    band_scores = jnp.einsum("nqd,nkd->nqk", band_q, band_k) * factor
    shaped = band_scores.reshape(N_WB, tile_total, TILE, tile_total, TILE)
    band_scores = jnp.where(allowed[:, :, None, :, None], shaped, -jnp.inf).reshape(N_WB, tile_total * TILE, tile_total * TILE)
    zero_col = jnp.zeros_like(key_f[:, :1])
    left_keys = jnp.concatenate([zero_col, key_f[:, :-1]], axis=1)
    right_keys = jnp.concatenate([key_f[:, 1:], zero_col], axis=1)
    left_vals = jnp.concatenate([zero_col, value_f[:, :-1]], axis=1)
    right_vals = jnp.concatenate([value_f[:, 1:], zero_col], axis=1)
    column = jnp.arange(GC, dtype=jnp.int32)
    left_ok = (column % TC == 0) & (column >= 1) & (radius >= 1)
    right_ok = (column % TC == TC - 1) & (column <= GC - 2) & (radius >= 1)
    left_scores = jnp.einsum("rcid,rcjd->rcij", query_f, left_keys) * factor
    left_scores = jnp.where(left_ok[None, :, None, None], left_scores, -jnp.inf)
    right_scores = jnp.einsum("rcid,rcjd->rcij", query_f, right_keys) * factor
    right_scores = jnp.where(right_ok[None, :, None, None], right_scores, -jnp.inf)
    top = to_grid(jnp.max(band_scores, axis=-1))
    top = jnp.maximum(top, jnp.max(left_scores, axis=-1))
    top = jnp.maximum(top, jnp.max(right_scores, axis=-1))
    total = to_grid(jnp.sum(jnp.exp(band_scores - to_band(top)[..., None]), axis=-1))
    total = total + jnp.sum(jnp.exp(left_scores - top[..., None]), axis=-1)
    total = total + jnp.sum(jnp.exp(right_scores - top[..., None]), axis=-1)
    log_sum = top + jnp.log(total)
    band_probs = jnp.exp(band_scores - to_band(log_sum)[..., None])
    left_probs = jnp.exp(left_scores - log_sum[..., None])
    right_probs = jnp.exp(right_scores - log_sum[..., None])
    band_half = settle(band_probs)
    left_half = settle(left_probs)
    right_half = settle(right_probs)
    output = to_grid(jnp.einsum("nqk,nkd->nqd", band_half, band_v))
    output = output + jnp.einsum("rcij,rcjd->rcid", left_half, left_vals)
    output = output + jnp.einsum("rcij,rcjd->rcid", right_half, right_vals)
    delta = jnp.sum(cotan_f * output, axis=-1)
    band_slopes = jnp.einsum("nqd,nkd->nqk", band_d, band_v)
    band_grad = settle(band_probs * (band_slopes - to_band(delta)[..., None]) * factor)
    left_slopes = jnp.einsum("rcid,rcjd->rcij", cotan_f, left_vals)
    left_grad = settle(left_probs * (left_slopes - delta[..., None]) * factor)
    right_slopes = jnp.einsum("rcid,rcjd->rcij", cotan_f, right_vals)
    right_grad = settle(right_probs * (right_slopes - delta[..., None]) * factor)
    grad_q = to_grid(jnp.einsum("nqk,nkd->nqd", band_grad, band_k))
    grad_q = grad_q + jnp.einsum("rcij,rcjd->rcid", left_grad, left_keys)
    grad_q = grad_q + jnp.einsum("rcij,rcjd->rcid", right_grad, right_keys)
    dev_rows = TR * TC * TILE
    grad_groups = band_grad.reshape(N_WB, N_HB, dev_rows, tile_total * TILE)
    half_groups = band_half.reshape(N_WB, N_HB, dev_rows, tile_total * TILE)
    query_groups = band_q.reshape(N_WB, N_HB, dev_rows, HD)
    cotan_groups = band_d.reshape(N_WB, N_HB, dev_rows, HD)
    key_band = jnp.sum(settle(jnp.einsum("ngqk,ngqd->ngkd", grad_groups, query_groups)), axis=1)
    value_band = jnp.sum(settle(jnp.einsum("ngqk,ngqd->ngkd", half_groups, cotan_groups)), axis=1)
    zero_grid = jnp.zeros_like(query_f[:, :1])
    left_key = jnp.einsum("rcij,rcid->rcjd", left_grad, query_f)
    right_key = jnp.einsum("rcij,rcid->rcjd", right_grad, query_f)
    left_value = jnp.einsum("rcij,rcid->rcjd", left_half, cotan_f)
    right_value = jnp.einsum("rcij,rcid->rcjd", right_half, cotan_f)
    grad_k = to_grid(key_band) + jnp.concatenate([left_key[:, 1:], zero_grid], axis=1) + jnp.concatenate([zero_grid, right_key[:, :-1]], axis=1)
    grad_v = to_grid(value_band) + jnp.concatenate([left_value[:, 1:], zero_grid], axis=1) + jnp.concatenate([zero_grid, right_value[:, :-1]], axis=1)
    return grad_q.astype(jnp.bfloat16), grad_k.astype(jnp.bfloat16), grad_v.astype(jnp.bfloat16)


def reference(query_rows, key_rows, value_rows, grad_out, sel_tiles, sel_count, tile_radius):
    band_sel = jnp.moveaxis(sel_tiles.reshape(GR, N_WB, TC, SEL), 1, 0)
    band_count = jnp.moveaxis(sel_count.reshape(GR, N_WB, TC), 1, 0)

    def band_mask(picked, counted):
        return tile_masks(tile_radius, picked, counted)

    allowed = jnp.moveaxis(jax.vmap(band_mask)(band_sel, band_count), 1, 0)

    def per_head(items):
        return head_grads(items[0], items[1], items[2], items[3], items[4], items[5])

    grad_query, grad_key, grad_value = lax.map(per_head, (query_rows, key_rows, value_rows, grad_out, tile_radius, allowed))
    return grad_query, grad_key, grad_value
```

```python
import functools

import jax
import jax.numpy as jnp
from jax import lax
from jax.experimental import pallas as pl
from jax.experimental.pallas import tpu as pltpu
from jax.sharding import PartitionSpec as P

CLOSED = -1e30
STAT_ROWS = 16
NT = (((1,), (1,)), ((), ()))
NN = (((1,), (0,)), ((), ()))


def dot(a, b, dims):
    return lax.dot_general(a, b, dims, preferred_element_type=jnp.float32)


def three_terms(x):
    high = x.astype(jnp.bfloat16).astype(jnp.float32)
    rest = x - high
    mid = rest.astype(jnp.bfloat16).astype(jnp.float32)
    return [high, mid, rest - mid]


def as_row(col):
    n = col.shape[0]
    return jnp.transpose(jnp.broadcast_to(col, (n, n)))[0:1]


def query_side(
    edge_ref, keys_ref, values_ref, q_ref, g_ref, left_ref, right_ref, bias_ref,
    dq_ref, sent_ref, stats_ref, *, factor, tile
):
    head = pl.program_id(0)
    rows, dim = q_ref.shape[1:]
    keys = keys_ref[:, 0, 0].reshape(-1, dim)
    values = values_ref[:, 0, 0].reshape(-1, dim)
    q = q_ref[0]
    g = g_ref[0]
    shaped = (rows // tile, tile, keys.shape[0])
    scores = dot(q, keys, NT) * factor
    scores = (scores.reshape(shaped) + bias_ref[0][:, None, :]).reshape(rows, -1)
    edge_keys = (left_ref[0, 0], right_ref[0, 0])
    edge_values = (left_ref[1, 0], right_ref[1, 0])
    edge_q = (q[:tile], q[rows - tile:])
    edge_g = (g[:tile], g[rows - tile:])
    edge_scores = [
        dot(edge_q[i], edge_keys[i], NT) * factor + edge_ref[head, i] for i in range(2)
    ]
    inner = rows - 2 * tile

    def spread(parts, fill):
        mid = [jnp.full((inner, 1), fill, jnp.float32)] if inner else []
        return jnp.concatenate([parts[0]] + mid + [parts[1]], axis=0)

    def own(x, i):
        return x[:tile] if i == 0 else x[rows - tile:]

    edge_top = spread([jnp.max(e, axis=1, keepdims=True) for e in edge_scores], CLOSED)
    top = jnp.maximum(jnp.max(scores, axis=1, keepdims=True), edge_top)
    powers = jnp.exp(scores - top)
    edge_powers = [jnp.exp(edge_scores[i] - own(top, i)) for i in range(2)]
    total = jnp.sum(powers, axis=1, keepdims=True) + spread(
        [jnp.sum(e, axis=1, keepdims=True) for e in edge_powers], 0.0
    )
    scale = 1.0 / total
    probs = powers * scale
    edge_probs = [edge_powers[i] * own(scale, i) for i in range(2)]
    slopes = dot(g, values, NT)
    edge_slopes = [dot(edge_g[i], edge_values[i], NT) for i in range(2)]

    def half(x):
        return x.astype(jnp.bfloat16).astype(jnp.float32)

    delta = jnp.sum(half(probs) * slopes, axis=1, keepdims=True) + spread(
        [
            jnp.sum(half(edge_probs[i]) * edge_slopes[i], axis=1, keepdims=True)
            for i in range(2)
        ],
        0.0,
    )
    grad = (probs * (slopes - delta) * factor).astype(jnp.bfloat16)
    dq = dot(grad, keys, NN)
    edge_dq = []
    for i in range(2):
        part = edge_probs[i] * (edge_slopes[i] - own(delta, i)) * factor
        edge_dq.append(dot(part.astype(jnp.bfloat16), edge_keys[i], NN))
    dq_ref[0, :tile] = (dq[:tile] + edge_dq[0]).astype(jnp.bfloat16)
    if inner:
        dq_ref[0, tile:rows - tile] = dq[tile:rows - tile].astype(jnp.bfloat16)
    dq_ref[0, rows - tile:] = (dq[rows - tile:] + edge_dq[1]).astype(jnp.bfloat16)
    log_row = as_row(top + jnp.log(total))
    delta_row = as_row(delta)
    pieces = three_terms(log_row) + three_terms(delta_row)
    blank = jnp.zeros((STAT_ROWS - len(pieces), rows), jnp.float32)
    sent_ref[0, :rows] = g
    sent_ref[0, rows:] = jnp.concatenate(pieces + [blank], axis=0).astype(jnp.bfloat16)
    stats_ref[0] = jnp.concatenate(
        [log_row, delta_row, jnp.zeros((6, rows), jnp.float32)], axis=0
    )


def key_side(
    edge_ref, queries_ref, sent_ref, k_ref, v_ref, left_ref, right_ref,
    left_stats_ref, right_stats_ref, bias_ref, dk_ref, dv_ref, *, factor, tile
):
    head = pl.program_id(0)
    rows, dim = k_ref.shape[1:]
    bands = queries_ref.shape[0]
    queries = queries_ref[:, 0, 0].reshape(-1, dim)
    cotan = sent_ref[:, 0, :rows].reshape(-1, dim)
    k = k_ref[0]
    v = v_ref[0]
    terms = sent_ref[:, 0, rows:].astype(jnp.float32)
    log_sum = terms[:, 0] + terms[:, 1] + terms[:, 2]
    delta = terms[:, 3] + terms[:, 4] + terms[:, 5]
    scores = dot(k, queries, NT)
    slopes = dot(v, cotan, NT)
    grads, probs = [], []
    tiles = rows // tile
    for r in range(bands):
        at = slice(r * rows, (r + 1) * rows)
        offset = bias_ref[0][:, at] - log_sum[r:r + 1]
        part = (scores[:, at] * factor).reshape(tiles, tile, rows) + offset[:, None, :]
        prob = jnp.exp(part).reshape(rows, rows)
        probs.append(prob.astype(jnp.bfloat16))
        grads.append((prob * (slopes[:, at] - delta[r:r + 1]) * factor).astype(jnp.bfloat16))
    dk = dot(jnp.concatenate(grads, axis=1), queries, NN)
    dv = dot(jnp.concatenate(probs, axis=1), cotan, NN)
    edge_k = (k[:tile], k[rows - tile:])
    edge_v = (v[:tile], v[rows - tile:])
    edge_stats = (left_stats_ref[0][:, rows - tile:], right_stats_ref[0][:, :tile])
    halos = (left_ref, right_ref)
    edge_dk, edge_dv = [], []
    for i in range(2):
        q_edge = halos[i][2, 0]
        g_edge = halos[i][3, 0]
        stats = edge_stats[i]
        part = dot(edge_k[i], q_edge, NT) * factor + (edge_ref[head, i] - stats[0:1])
        prob = jnp.exp(part)
        grad = prob * (dot(edge_v[i], g_edge, NT) - stats[1:2]) * factor
        edge_dk.append(dot(grad.astype(jnp.bfloat16), q_edge, NN))
        edge_dv.append(dot(prob.astype(jnp.bfloat16), g_edge, NN))
    for ref, whole, edge in ((dk_ref, dk, edge_dk), (dv_ref, dv, edge_dv)):
        ref[0, :tile] = (whole[:tile] + edge[0]).astype(jnp.bfloat16)
        if rows > 2 * tile:
            ref[0, tile:rows - tile] = whole[tile:rows - tile].astype(jnp.bfloat16)
        ref[0, rows - tile:] = (whole[rows - tile:] + edge[1]).astype(jnp.bfloat16)


def tile_masks(tile_radius, sel_tiles, sel_count):
    band_rows, band_cols, picks = sel_tiles.shape
    tile_total = band_rows * band_cols
    tile_index = jnp.arange(tile_total, dtype=jnp.int32)
    row_of = tile_index // band_cols
    col_of = tile_index % band_cols
    spread = jnp.abs(row_of[:, None] - row_of[None, :]) + jnp.abs(col_of[:, None] - col_of[None, :])
    nearby = spread[None] <= tile_radius[:, None, None]
    live_pick = jnp.arange(picks, dtype=jnp.int32)[None, :] < sel_count.reshape(tile_total, 1)
    matches = (sel_tiles.reshape(tile_total, picks, 1) == tile_index[None, None, :]) & live_pick[
        :, :, None
    ]
    return nearby | jnp.any(matches, axis=1)[None]


def neighbours(first, last, axis):
    size = lax.axis_size(axis)
    up = [(i, i + 1) for i in range(size - 1)]
    down = [(i + 1, i) for i in range(size - 1)]
    return lax.ppermute(last, axis, up), lax.ppermute(first, axis, down)


def row_bias(allowed, tile):
    bias = jnp.where(allowed, 0.0, CLOSED).astype(jnp.float32)
    heads, own, others = bias.shape
    wide = jnp.broadcast_to(bias[..., None], (heads, own, others, tile))
    return wide.reshape(heads, own, others * tile)


def on_device(query_rows, key_rows, value_rows, grad_out, sel_tiles, sel_count, tile_radius):
    heads, tile_rows, tile_cols, tile, dim = query_rows.shape
    dev_tiles = tile_rows * tile_cols
    rows = dev_tiles * tile
    factor = dim ** (-0.5)
    hb_index = lax.axis_index("hb")
    wb_index = lax.axis_index("wb")
    bands = lax.axis_size("hb")
    flat = (heads, rows, dim)
    q, k, v, g = (x.reshape(flat) for x in (query_rows, key_rows, value_rows, grad_out))
    kv = lax.all_gather(jnp.stack((k, v)), "hb")
    all_q = lax.all_gather(q[None], "hb")
    four = (k, v, q, g)
    left, right = neighbours(
        jnp.stack([x[:, :tile] for x in four]), jnp.stack([x[:, rows - tile:] for x in four]), "wb"
    )
    allowed = tile_masks(tile_radius, sel_tiles, sel_count)
    start = hb_index * dev_tiles
    own_bias = row_bias(lax.dynamic_slice_in_dim(allowed, start, dev_tiles, 1), tile)
    col_bias = row_bias(
        jnp.swapaxes(lax.dynamic_slice_in_dim(allowed, start, dev_tiles, 2), 1, 2), tile
    )
    reach = tile_radius >= 1
    edge_open = jnp.stack(
        (reach & (wb_index >= 1), reach & (wb_index < lax.axis_size("wb") - 1)), axis=1
    )
    edge_bias = jnp.where(edge_open, 0.0, CLOSED).astype(jnp.float32)

    def per_head(shape):
        return pl.BlockSpec((1,) + shape, lambda h: (h,) + (0,) * len(shape))

    smem = pl.BlockSpec(memory_space=pltpu.SMEM)
    own = per_head((rows, dim))
    halo = pl.BlockSpec((4, 1, tile, dim), lambda h: (0, h, 0, 0))
    bias = per_head((dev_tiles, bands * rows))
    stat = per_head((8, rows))
    sent_shape = (rows + STAT_ROWS, dim)
    half = functools.partial(jax.ShapeDtypeStruct, dtype=jnp.bfloat16)
    dq, sent, stats = pl.pallas_call(
        functools.partial(query_side, factor=factor, tile=tile),
        grid=(heads,),
        in_specs=[
            smem,
            pl.BlockSpec((bands, 1, 1, rows, dim), lambda h: (0, 0, h, 0, 0)),
            pl.BlockSpec((bands, 1, 1, rows, dim), lambda h: (0, 1, h, 0, 0)),
            own, own, halo, halo, bias,
        ],
        out_specs=[own, per_head(sent_shape), stat],
        out_shape=[
            half(flat), half((heads,) + sent_shape),
            jax.ShapeDtypeStruct((heads, 8, rows), jnp.float32),
        ],
        name="query_side",
    )(edge_bias, kv, kv, q, g, left, right, own_bias)
    all_sent = lax.all_gather(sent, "hb")
    left_stats, right_stats = neighbours(stats, stats, "wb")
    dk, dv = pl.pallas_call(
        functools.partial(key_side, factor=factor, tile=tile),
        grid=(heads,),
        in_specs=[
            smem,
            pl.BlockSpec((bands, 1, 1, rows, dim), lambda h: (0, 0, h, 0, 0)),
            pl.BlockSpec((bands, 1) + sent_shape, lambda h: (0, h, 0, 0)),
            own, own, halo, halo, stat, stat, bias,
        ],
        out_specs=[own, own],
        out_shape=[half(flat), half(flat)],
        name="key_side",
    )(edge_bias, all_q, all_sent, k, v, left, right, left_stats, right_stats, col_bias)
    return tuple(x.reshape(query_rows.shape) for x in (dq, dk, dv))


def solution(mesh):
    banded = P("hd", "hb", "wb", None, None)
    return jax.shard_map(
        on_device,
        mesh=mesh,
        in_specs=(banded,) * 4 + (P(None, "wb", None), P(None, "wb"), P("hd")),
        out_specs=(banded,) * 3,
        check_vma=False,
    )
```

```python
import functools

import jax
import jax.numpy as jnp
from jax import lax
from jax.experimental import pallas as pl
from jax.experimental.pallas import tpu as pltpu
from jax.sharding import PartitionSpec as P

CLOSED = -1e30
NT = (((1,), (1,)), ((), ()))
NN = (((1,), (0,)), ((), ()))


def dot(a, b, dims):
    return lax.dot_general(a, b, dims, preferred_element_type=jnp.float32)


def as_row(col):
    n = col.shape[0]
    return jnp.transpose(jnp.broadcast_to(col, (n, n)))[0:1]


def query_side(
    edge_ref, keys_ref, values_ref, q_ref, g_ref, left_ref, right_ref, bias_ref,
    dq_ref, stats_ref, *, factor, tile
):
    head = pl.program_id(0)
    rows, dim = q_ref.shape[1:]
    keys = keys_ref[:, 0, 0].reshape(-1, dim)
    values = values_ref[:, 0, 0].reshape(-1, dim)
    q = q_ref[0]
    g = g_ref[0]
    shaped = (rows // tile, tile, keys.shape[0])
    scores = dot(q, keys, NT) * factor
    scores = (scores.reshape(shaped) + bias_ref[0][:, None, :]).reshape(rows, -1)
    edge_keys = (left_ref[0, 0], right_ref[0, 0])
    edge_values = (left_ref[1, 0], right_ref[1, 0])
    edge_q = (q[:tile], q[rows - tile:])
    edge_g = (g[:tile], g[rows - tile:])
    edge_scores = [
        dot(edge_q[i], edge_keys[i], NT) * factor + edge_ref[head, i] for i in range(2)
    ]
    inner = rows - 2 * tile

    def spread(parts, fill):
        mid = [jnp.full((inner, 1), fill, jnp.float32)] if inner else []
        return jnp.concatenate([parts[0]] + mid + [parts[1]], axis=0)

    def own(x, i):
        return x[:tile] if i == 0 else x[rows - tile:]

    edge_top = spread([jnp.max(e, axis=1, keepdims=True) for e in edge_scores], CLOSED)
    top = jnp.maximum(jnp.max(scores, axis=1, keepdims=True), edge_top)
    powers = jnp.exp(scores - top)
    edge_powers = [jnp.exp(edge_scores[i] - own(top, i)) for i in range(2)]
    total = jnp.sum(powers, axis=1, keepdims=True) + spread(
        [jnp.sum(e, axis=1, keepdims=True) for e in edge_powers], 0.0
    )
    scale = 1.0 / total
    probs = powers * scale
    edge_probs = [edge_powers[i] * own(scale, i) for i in range(2)]
    slopes = dot(g, values, NT)
    edge_slopes = [dot(edge_g[i], edge_values[i], NT) for i in range(2)]

    def half(x):
        return x.astype(jnp.bfloat16).astype(jnp.float32)

    delta = jnp.sum(half(probs) * slopes, axis=1, keepdims=True) + spread(
        [
            jnp.sum(half(edge_probs[i]) * edge_slopes[i], axis=1, keepdims=True)
            for i in range(2)
        ],
        0.0,
    )
    grad = (probs * (slopes - delta) * factor).astype(jnp.bfloat16)
    dq = dot(grad, keys, NN)
    edge_dq = []
    for i in range(2):
        part = edge_probs[i] * (edge_slopes[i] - own(delta, i)) * factor
        edge_dq.append(dot(part.astype(jnp.bfloat16), edge_keys[i], NN))
    dq_ref[0, :tile] = (dq[:tile] + edge_dq[0]).astype(jnp.bfloat16)
    if inner:
        dq_ref[0, tile:rows - tile] = dq[tile:rows - tile].astype(jnp.bfloat16)
    dq_ref[0, rows - tile:] = (dq[rows - tile:] + edge_dq[1]).astype(jnp.bfloat16)
    stats_ref[0, 0:1] = as_row(top + jnp.log(total))
    stats_ref[0, 1:2] = as_row(delta)


def key_side(
    edge_ref, queries_ref, cotan_ref, all_stats_ref, k_ref, v_ref, left_ref, right_ref,
    left_stats_ref, right_stats_ref, bias_ref, dk_ref, dv_ref, *, factor, tile
):
    head = pl.program_id(0)
    rows, dim = k_ref.shape[1:]
    bands = queries_ref.shape[0]
    queries = queries_ref[:, 0, 0].reshape(-1, dim)
    cotan = cotan_ref[:, 0, 0].reshape(-1, dim)
    k = k_ref[0]
    v = v_ref[0]
    scores = dot(k, queries, NT)
    slopes = dot(v, cotan, NT)
    grads, probs = [], []
    tiles = rows // tile
    for r in range(bands):
        at = slice(r * rows, (r + 1) * rows)
        offset = bias_ref[0][:, at] - all_stats_ref[r, 0, 0:1]
        part = (scores[:, at] * factor).reshape(tiles, tile, rows) + offset[:, None, :]
        prob = jnp.exp(part).reshape(rows, rows)
        probs.append(prob.astype(jnp.bfloat16))
        grads.append((prob * (slopes[:, at] - all_stats_ref[r, 0, 1:2]) * factor).astype(jnp.bfloat16))
    dk = dot(jnp.concatenate(grads, axis=1), queries, NN)
    dv = dot(jnp.concatenate(probs, axis=1), cotan, NN)
    edge_k = (k[:tile], k[rows - tile:])
    edge_v = (v[:tile], v[rows - tile:])
    edge_stats = (left_stats_ref[0][:, rows - tile:], right_stats_ref[0][:, :tile])
    halos = (left_ref, right_ref)
    edge_dk, edge_dv = [], []
    for i in range(2):
        q_edge = halos[i][2, 0]
        g_edge = halos[i][3, 0]
        stats = edge_stats[i]
        part = dot(edge_k[i], q_edge, NT) * factor + (edge_ref[head, i] - stats[0:1])
        prob = jnp.exp(part)
        grad = prob * (dot(edge_v[i], g_edge, NT) - stats[1:2]) * factor
        edge_dk.append(dot(grad.astype(jnp.bfloat16), q_edge, NN))
        edge_dv.append(dot(prob.astype(jnp.bfloat16), g_edge, NN))
    for ref, whole, edge in ((dk_ref, dk, edge_dk), (dv_ref, dv, edge_dv)):
        ref[0, :tile] = (whole[:tile] + edge[0]).astype(jnp.bfloat16)
        if rows > 2 * tile:
            ref[0, tile:rows - tile] = whole[tile:rows - tile].astype(jnp.bfloat16)
        ref[0, rows - tile:] = (whole[rows - tile:] + edge[1]).astype(jnp.bfloat16)


def tile_masks(tile_radius, sel_tiles, sel_count):
    band_rows, band_cols, picks = sel_tiles.shape
    tile_total = band_rows * band_cols
    tile_index = jnp.arange(tile_total, dtype=jnp.int32)
    row_of = tile_index // band_cols
    col_of = tile_index % band_cols
    spread = jnp.abs(row_of[:, None] - row_of[None, :]) + jnp.abs(col_of[:, None] - col_of[None, :])
    nearby = spread[None] <= tile_radius[:, None, None]
    live_pick = jnp.arange(picks, dtype=jnp.int32)[None, :] < sel_count.reshape(tile_total, 1)
    matches = (sel_tiles.reshape(tile_total, picks, 1) == tile_index[None, None, :]) & live_pick[
        :, :, None
    ]
    return nearby | jnp.any(matches, axis=1)[None]


def neighbours(first, last, axis):
    size = lax.axis_size(axis)
    up = [(i, i + 1) for i in range(size - 1)]
    down = [(i + 1, i) for i in range(size - 1)]
    return lax.ppermute(last, axis, up), lax.ppermute(first, axis, down)


def row_bias(allowed, tile):
    bias = jnp.where(allowed, 0.0, CLOSED).astype(jnp.float32)
    heads, own, others = bias.shape
    wide = jnp.broadcast_to(bias[..., None], (heads, own, others, tile))
    return wide.reshape(heads, own, others * tile)


def on_device(query_rows, key_rows, value_rows, grad_out, sel_tiles, sel_count, tile_radius):
    heads, tile_rows, tile_cols, tile, dim = query_rows.shape
    dev_tiles = tile_rows * tile_cols
    rows = dev_tiles * tile
    factor = dim ** (-0.5)
    hb_index = lax.axis_index("hb")
    wb_index = lax.axis_index("wb")
    bands = lax.axis_size("hb")
    flat = (heads, rows, dim)
    q, k, v, g = (x.reshape(flat) for x in (query_rows, key_rows, value_rows, grad_out))
    four = (k, v, q, g)
    band = lax.all_gather(jnp.stack(four), "hb")
    left, right = neighbours(
        jnp.stack([x[:, :tile] for x in four]), jnp.stack([x[:, rows - tile:] for x in four]), "wb"
    )
    allowed = tile_masks(tile_radius, sel_tiles, sel_count)
    start = hb_index * dev_tiles
    own_bias = row_bias(lax.dynamic_slice_in_dim(allowed, start, dev_tiles, 1), tile)
    col_bias = row_bias(
        jnp.swapaxes(lax.dynamic_slice_in_dim(allowed, start, dev_tiles, 2), 1, 2), tile
    )
    reach = tile_radius >= 1
    edge_open = jnp.stack(
        (reach & (wb_index >= 1), reach & (wb_index < lax.axis_size("wb") - 1)), axis=1
    )
    edge_bias = jnp.where(edge_open, 0.0, CLOSED).astype(jnp.float32)

    def per_head(shape):
        return pl.BlockSpec((1,) + shape, lambda h: (h,) + (0,) * len(shape))

    smem = pl.BlockSpec(memory_space=pltpu.SMEM)
    own = per_head((rows, dim))
    halo = pl.BlockSpec((4, 1, tile, dim), lambda h: (0, h, 0, 0))
    bias = per_head((dev_tiles, bands * rows))
    stat = per_head((2, rows))

    def of_band(slot):
        return pl.BlockSpec((bands, 1, 1, rows, dim), lambda h: (0, slot, h, 0, 0))

    half = functools.partial(jax.ShapeDtypeStruct, dtype=jnp.bfloat16)
    dq, stats = pl.pallas_call(
        functools.partial(query_side, factor=factor, tile=tile),
        grid=(heads,),
        in_specs=[
            smem,
            of_band(0), of_band(1), own, own, halo, halo, bias,
        ],
        out_specs=[own, stat],
        out_shape=[half(flat), jax.ShapeDtypeStruct((heads, 2, rows), jnp.float32)],
        name="query_side",
    )(edge_bias, band, band, q, g, left, right, own_bias)
    all_stats = lax.all_gather(stats, "hb")
    left_stats, right_stats = neighbours(stats, stats, "wb")
    dk, dv = pl.pallas_call(
        functools.partial(key_side, factor=factor, tile=tile),
        grid=(heads,),
        in_specs=[
            smem,
            of_band(2), of_band(3),
            pl.BlockSpec((bands, 1, 2, rows), lambda h: (0, h, 0, 0)),
            own, own, halo, halo, stat, stat, bias,
        ],
        out_specs=[own, own],
        out_shape=[half(flat), half(flat)],
        name="key_side",
    )(edge_bias, band, band, all_stats, k, v, left, right, left_stats, right_stats, col_bias)
    return tuple(x.reshape(query_rows.shape) for x in (dq, dk, dv))


def solution(mesh):
    banded = P("hd", "hb", "wb", None, None)
    return jax.shard_map(
        on_device,
        mesh=mesh,
        in_specs=(banded,) * 4 + (P(None, "wb", None), P(None, "wb"), P("hd")),
        out_specs=(banded,) * 3,
        check_vma=False,
    )
```

```python
import functools

import jax
import jax.numpy as jnp
from jax import lax
from jax.experimental import pallas as pl
from jax.experimental.pallas import tpu as pltpu
from jax.sharding import PartitionSpec as P

CLOSED = -1e30
NT = (((1,), (1,)), ((), ()))
NN = (((1,), (0,)), ((), ()))


def dot(a, b, dims):
    return lax.dot_general(a, b, dims, preferred_element_type=jnp.float32)


def as_row(col):
    n = col.shape[0]
    return jnp.transpose(jnp.broadcast_to(col, (n, n)))[0:1]


def joined(units, slot):
    return jnp.concatenate([u[i, slot, 0] for u in units for i in range(u.shape[0])], axis=0)


def bias_of(bias_ref, row, rows):
    return bias_ref[0, :, pl.ds(pl.multiple_of(row * rows, rows), rows)]


def query_side(order_ref, edge_ref, *refs, factor, tile):
    bands = order_ref.shape[0]
    units = refs[:-6]
    own_ref, left_ref, right_ref, bias_ref, dq_ref, stats_ref = refs[-6:]
    head = pl.program_id(0)
    rows, dim = dq_ref.shape[1:]
    keys = joined(units, 0)
    values = joined(units, 1)
    q = own_ref[0, 0]
    g = own_ref[1, 0]
    shaped = (rows // tile, tile, keys.shape[0])
    scores = dot(q, keys, NT) * factor
    bias = jnp.concatenate([bias_of(bias_ref, order_ref[u], rows) for u in range(bands)], axis=1)
    scores = (scores.reshape(shaped) + bias[:, None, :]).reshape(rows, -1)
    edge_keys = (left_ref[0, 0], right_ref[0, 0])
    edge_values = (left_ref[1, 0], right_ref[1, 0])
    edge_q = (q[:tile], q[rows - tile:])
    edge_g = (g[:tile], g[rows - tile:])
    edge_scores = [
        dot(edge_q[i], edge_keys[i], NT) * factor + edge_ref[head, i] for i in range(2)
    ]
    inner = rows - 2 * tile

    def spread(parts, fill):
        mid = [jnp.full((inner, 1), fill, jnp.float32)] if inner else []
        return jnp.concatenate([parts[0]] + mid + [parts[1]], axis=0)

    def own(x, i):
        return x[:tile] if i == 0 else x[rows - tile:]

    edge_top = spread([jnp.max(e, axis=1, keepdims=True) for e in edge_scores], CLOSED)
    top = jnp.maximum(jnp.max(scores, axis=1, keepdims=True), edge_top)
    powers = jnp.exp(scores - top)
    edge_powers = [jnp.exp(edge_scores[i] - own(top, i)) for i in range(2)]
    total = jnp.sum(powers, axis=1, keepdims=True) + spread(
        [jnp.sum(e, axis=1, keepdims=True) for e in edge_powers], 0.0
    )
    scale = 1.0 / total
    probs = powers * scale
    edge_probs = [edge_powers[i] * own(scale, i) for i in range(2)]
    slopes = dot(g, values, NT)
    edge_slopes = [dot(edge_g[i], edge_values[i], NT) for i in range(2)]

    def half(x):
        return x.astype(jnp.bfloat16).astype(jnp.float32)

    delta = jnp.sum(half(probs) * slopes, axis=1, keepdims=True) + spread(
        [
            jnp.sum(half(edge_probs[i]) * edge_slopes[i], axis=1, keepdims=True)
            for i in range(2)
        ],
        0.0,
    )
    grad = (probs * (slopes - delta) * factor).astype(jnp.bfloat16)
    dq = dot(grad, keys, NN)
    edge_dq = []
    for i in range(2):
        part = edge_probs[i] * (edge_slopes[i] - own(delta, i)) * factor
        edge_dq.append(dot(part.astype(jnp.bfloat16), edge_keys[i], NN))
    dq_ref[0, :tile] = (dq[:tile] + edge_dq[0]).astype(jnp.bfloat16)
    if inner:
        dq_ref[0, tile:rows - tile] = dq[tile:rows - tile].astype(jnp.bfloat16)
    dq_ref[0, rows - tile:] = (dq[rows - tile:] + edge_dq[1]).astype(jnp.bfloat16)
    stats_ref[0, 0:1] = as_row(top + jnp.log(total))
    stats_ref[0, 1:2] = as_row(delta)


def key_side(
    edge_ref, asked_ref, all_stats_ref, own_ref, left_ref, right_ref, left_stats_ref,
    right_stats_ref, bias_ref, dk_ref, dv_ref, *, factor, tile
):
    bands = asked_ref.shape[0]
    head = pl.program_id(0)
    rows, dim = dk_ref.shape[1:]
    queries = joined([asked_ref], 0)
    cotan = joined([asked_ref], 1)
    k = own_ref[0, 0]
    v = own_ref[1, 0]
    scores = dot(k, queries, NT)
    slopes = dot(v, cotan, NT)
    grads, probs = [], []
    tiles = rows // tile
    for r in range(bands):
        at = slice(r * rows, (r + 1) * rows)
        offset = bias_ref[0][:, at] - all_stats_ref[r, 0, 0:1]
        part = (scores[:, at] * factor).reshape(tiles, tile, rows) + offset[:, None, :]
        prob = jnp.exp(part).reshape(rows, rows)
        probs.append(prob.astype(jnp.bfloat16))
        grads.append((prob * (slopes[:, at] - all_stats_ref[r, 0, 1:2]) * factor).astype(jnp.bfloat16))
    dk = dot(jnp.concatenate(grads, axis=1), queries, NN)
    dv = dot(jnp.concatenate(probs, axis=1), cotan, NN)
    edge_k = (k[:tile], k[rows - tile:])
    edge_v = (v[:tile], v[rows - tile:])
    edge_stats = (left_stats_ref[0][:, rows - tile:], right_stats_ref[0][:, :tile])
    halos = (left_ref, right_ref)
    edge_dk, edge_dv = [], []
    for i in range(2):
        q_edge = halos[i][2, 0]
        g_edge = halos[i][3, 0]
        stats = edge_stats[i]
        part = dot(edge_k[i], q_edge, NT) * factor + (edge_ref[head, i] - stats[0:1])
        prob = jnp.exp(part)
        grad = prob * (dot(edge_v[i], g_edge, NT) - stats[1:2]) * factor
        edge_dk.append(dot(grad.astype(jnp.bfloat16), q_edge, NN))
        edge_dv.append(dot(prob.astype(jnp.bfloat16), g_edge, NN))
    for ref, whole, edge in ((dk_ref, dk, edge_dk), (dv_ref, dv, edge_dv)):
        ref[0, :tile] = (whole[:tile] + edge[0]).astype(jnp.bfloat16)
        if rows > 2 * tile:
            ref[0, tile:rows - tile] = whole[tile:rows - tile].astype(jnp.bfloat16)
        ref[0, rows - tile:] = (whole[rows - tile:] + edge[1]).astype(jnp.bfloat16)


def tile_masks(tile_radius, sel_tiles, sel_count):
    band_rows, band_cols, picks = sel_tiles.shape
    tile_total = band_rows * band_cols
    tile_index = jnp.arange(tile_total, dtype=jnp.int32)
    row_of = tile_index // band_cols
    col_of = tile_index % band_cols
    spread = jnp.abs(row_of[:, None] - row_of[None, :]) + jnp.abs(col_of[:, None] - col_of[None, :])
    nearby = spread[None] <= tile_radius[:, None, None]
    live_pick = jnp.arange(picks, dtype=jnp.int32)[None, :] < sel_count.reshape(tile_total, 1)
    matches = (sel_tiles.reshape(tile_total, picks, 1) == tile_index[None, None, :]) & live_pick[
        :, :, None
    ]
    return nearby | jnp.any(matches, axis=1)[None]


def neighbours(first, last, axis):
    size = lax.axis_size(axis)
    up = [(i, i + 1) for i in range(size - 1)]
    down = [(i + 1, i) for i in range(size - 1)]
    return lax.ppermute(last, axis, up), lax.ppermute(first, axis, down)


def band_units(own, axis, aside):
    size = lax.axis_size(axis)
    index = lax.axis_index(axis)
    pairs = size // 2
    side = index % 2
    swap = [(i, i ^ 1) for i in range(size)]
    step = [(i, (i + (2 if i % 2 == 0 else -2)) % size) for i in range(size)]

    def handed(x):
        return lax.ppermute(x, axis, swap)

    def passed(x):
        return lax.ppermute(x, axis, step)

    held = jnp.stack((own, handed(own)))
    units, order = [held], [index, index ^ 1]
    for s in range(1, pairs // 2 + 1):
        if s == 3:
            held, aside = lax.optimization_barrier((held, aside))
        near = (index // 2 - (1 - 2 * side) * s) % pairs
        far = (index // 2 + (1 - 2 * side) * s) % pairs
        sides = [side, 1 - side]
        if 2 * s == pairs:
            held, sides = held[:1], sides[:1]
        held = passed(held)
        units += [held, handed(held)]
        order += [2 * near + i for i in sides] + [2 * far + 1 - i for i in sides]
    return units, jnp.stack(order).astype(jnp.int32), aside


def row_bias(allowed, tile):
    bias = jnp.where(allowed, 0.0, CLOSED).astype(jnp.float32)
    heads, own, others = bias.shape
    wide = jnp.broadcast_to(bias[..., None], (heads, own, others, tile))
    return wide.reshape(heads, own, others * tile)


def on_device(query_rows, key_rows, value_rows, grad_out, sel_tiles, sel_count, tile_radius):
    heads, tile_rows, tile_cols, tile, dim = query_rows.shape
    dev_tiles = tile_rows * tile_cols
    rows = dev_tiles * tile
    factor = dim ** (-0.5)
    hb_index = lax.axis_index("hb")
    wb_index = lax.axis_index("wb")
    bands = lax.axis_size("hb")
    flat = (heads, rows, dim)
    q, k, v, g = (x.reshape(flat) for x in (query_rows, key_rows, value_rows, grad_out))
    asking = jnp.stack((q, g))
    keyed = jnp.stack((k, v))
    all_asking = lax.all_gather(asking, "hb")
    four = (k, v, q, g)
    left, right = neighbours(
        jnp.stack([x[:, :tile] for x in four]), jnp.stack([x[:, rows - tile:] for x in four]), "wb"
    )
    allowed = tile_masks(tile_radius, sel_tiles, sel_count)
    start = hb_index * dev_tiles
    own_bias = row_bias(lax.dynamic_slice_in_dim(allowed, start, dev_tiles, 1), tile)
    col_bias = row_bias(
        jnp.swapaxes(lax.dynamic_slice_in_dim(allowed, start, dev_tiles, 2), 1, 2), tile
    )
    reach = tile_radius >= 1
    edge_open = jnp.stack(
        (reach & (wb_index >= 1), reach & (wb_index < lax.axis_size("wb") - 1)), axis=1
    )
    edge_bias = jnp.where(edge_open, 0.0, CLOSED).astype(jnp.float32)

    units, order, (own_bias, col_bias, edge_bias) = band_units(
        keyed, "hb", (own_bias, col_bias, edge_bias)
    )

    def per_head(shape):
        return pl.BlockSpec((1,) + shape, lambda h: (h,) + (0,) * len(shape))

    smem = pl.BlockSpec(memory_space=pltpu.SMEM)
    result = per_head((rows, dim))
    pair = pl.BlockSpec((2, 1, rows, dim), lambda h: (0, h, 0, 0))

    def units_of(count):
        return pl.BlockSpec((count, 2, 1, rows, dim), lambda h: (0, 0, h, 0, 0))

    halo = pl.BlockSpec((4, 1, tile, dim), lambda h: (0, h, 0, 0))
    bias = per_head((dev_tiles, bands * rows))
    stat = per_head((2, rows))
    half = jax.ShapeDtypeStruct(flat, jnp.bfloat16)
    dq, stats = pl.pallas_call(
        functools.partial(query_side, factor=factor, tile=tile),
        grid=(heads,),
        in_specs=[smem, smem] + [units_of(u.shape[0]) for u in units] + [pair, halo, halo, bias],
        out_specs=[result, stat],
        out_shape=[half, jax.ShapeDtypeStruct((heads, 2, rows), jnp.float32)],
        name="query_side",
    )(order, edge_bias, *units, asking, left, right, own_bias)
    left_stats, right_stats = neighbours(stats, stats, "wb")
    all_stats = lax.all_gather(stats, "hb")
    dk, dv = pl.pallas_call(
        functools.partial(key_side, factor=factor, tile=tile),
        grid=(heads,),
        in_specs=[
            smem, units_of(bands),
            pl.BlockSpec((bands, 1, 2, rows), lambda h: (0, h, 0, 0)),
            pair, halo, halo, stat, stat, bias,
        ],
        out_specs=[result, result],
        out_shape=[half, half],
        name="key_side",
    )(
        edge_bias, all_asking, all_stats, keyed, left, right, left_stats, right_stats, col_bias
    )
    return tuple(x.reshape(query_rows.shape) for x in (dq, dk, dv))


def solution(mesh):
    banded = P("hd", "hb", "wb", None, None)
    return jax.shard_map(
        on_device,
        mesh=mesh,
        in_specs=(banded,) * 4 + (P(None, "wb", None), P(None, "wb"), P("hd")),
        out_specs=(banded,) * 3,
        check_vma=False,
    )
```

```python
import functools

import jax
import jax.numpy as jnp
from jax import lax
from jax.experimental import pallas as pl
from jax.experimental.pallas import tpu as pltpu
from jax.sharding import PartitionSpec as P

CLOSED = -1e30
NT = (((1,), (1,)), ((), ()))
NN = (((1,), (0,)), ((), ()))


def dot(a, b, dims):
    return lax.dot_general(a, b, dims, preferred_element_type=jnp.float32)


def as_row(col):
    n = col.shape[0]
    return jnp.transpose(jnp.broadcast_to(col, (n, n)))[0:1]


def joined(units, slot):
    return jnp.concatenate([u[i, slot, 0] for u in units for i in range(u.shape[0])], axis=0)


def bias_of(bias_ref, row, rows):
    return bias_ref[0, :, pl.ds(pl.multiple_of(row * rows, rows), rows)]


def query_side(order_ref, edge_ref, *refs, factor, tile):
    bands = order_ref.shape[0]
    units = refs[:-6]
    own_ref, left_ref, right_ref, bias_ref, dq_ref, stats_ref = refs[-6:]
    head = pl.program_id(0)
    rows, dim = dq_ref.shape[1:]
    keys = joined(units, 0)
    values = joined(units, 1)
    q = own_ref[0, 0]
    g = own_ref[1, 0]
    shaped = (rows // tile, tile, keys.shape[0])
    scores = dot(q, keys, NT) * factor
    bias = jnp.concatenate([bias_of(bias_ref, order_ref[u], rows) for u in range(bands)], axis=1)
    scores = (scores.reshape(shaped) + bias[:, None, :]).reshape(rows, -1)
    edge_keys = (left_ref[0, 0], right_ref[0, 0])
    edge_values = (left_ref[1, 0], right_ref[1, 0])
    edge_q = (q[:tile], q[rows - tile:])
    edge_g = (g[:tile], g[rows - tile:])
    edge_scores = [
        dot(edge_q[i], edge_keys[i], NT) * factor + edge_ref[head, i] for i in range(2)
    ]
    inner = rows - 2 * tile

    def spread(parts, fill):
        mid = [jnp.full((inner, 1), fill, jnp.float32)] if inner else []
        return jnp.concatenate([parts[0]] + mid + [parts[1]], axis=0)

    def own(x, i):
        return x[:tile] if i == 0 else x[rows - tile:]

    edge_top = spread([jnp.max(e, axis=1, keepdims=True) for e in edge_scores], CLOSED)
    top = jnp.maximum(jnp.max(scores, axis=1, keepdims=True), edge_top)
    powers = jnp.exp(scores - top)
    edge_powers = [jnp.exp(edge_scores[i] - own(top, i)) for i in range(2)]
    total = jnp.sum(powers, axis=1, keepdims=True) + spread(
        [jnp.sum(e, axis=1, keepdims=True) for e in edge_powers], 0.0
    )
    scale = 1.0 / total
    probs = powers * scale
    edge_probs = [edge_powers[i] * own(scale, i) for i in range(2)]
    slopes = dot(g, values, NT)
    edge_slopes = [dot(edge_g[i], edge_values[i], NT) for i in range(2)]

    def half(x):
        return x.astype(jnp.bfloat16).astype(jnp.float32)

    delta = jnp.sum(half(probs) * slopes, axis=1, keepdims=True) + spread(
        [
            jnp.sum(half(edge_probs[i]) * edge_slopes[i], axis=1, keepdims=True)
            for i in range(2)
        ],
        0.0,
    )
    grad = (probs * (slopes - delta) * factor).astype(jnp.bfloat16)
    dq = dot(grad, keys, NN)
    edge_dq = []
    for i in range(2):
        part = edge_probs[i] * (edge_slopes[i] - own(delta, i)) * factor
        edge_dq.append(dot(part.astype(jnp.bfloat16), edge_keys[i], NN))
    dq_ref[0, :tile] = (dq[:tile] + edge_dq[0]).astype(jnp.bfloat16)
    if inner:
        dq_ref[0, tile:rows - tile] = dq[tile:rows - tile].astype(jnp.bfloat16)
    dq_ref[0, rows - tile:] = (dq[rows - tile:] + edge_dq[1]).astype(jnp.bfloat16)
    stats_ref[0, 0:1] = as_row(top + jnp.log(total))
    stats_ref[0, 1:2] = as_row(delta)


def key_side(
    edge_ref, asked_ref, all_stats_ref, own_ref, left_ref, right_ref, left_stats_ref,
    right_stats_ref, bias_ref, dk_ref, dv_ref, *, factor, tile
):
    bands = asked_ref.shape[0]
    head = pl.program_id(0)
    rows, dim = dk_ref.shape[1:]
    queries = joined([asked_ref], 0)
    cotan = joined([asked_ref], 1)
    k = own_ref[0, 0]
    v = own_ref[1, 0]
    scores = dot(k, queries, NT)
    slopes = dot(v, cotan, NT)
    grads, probs = [], []
    tiles = rows // tile
    for r in range(bands):
        at = slice(r * rows, (r + 1) * rows)
        offset = bias_ref[0][:, at] - all_stats_ref[r, 0, 0:1]
        part = (scores[:, at] * factor).reshape(tiles, tile, rows) + offset[:, None, :]
        prob = jnp.exp(part).reshape(rows, rows)
        probs.append(prob.astype(jnp.bfloat16))
        grads.append((prob * (slopes[:, at] - all_stats_ref[r, 0, 1:2]) * factor).astype(jnp.bfloat16))
    dk = dot(jnp.concatenate(grads, axis=1), queries, NN)
    dv = dot(jnp.concatenate(probs, axis=1), cotan, NN)
    edge_k = (k[:tile], k[rows - tile:])
    edge_v = (v[:tile], v[rows - tile:])
    edge_stats = (left_stats_ref[0][:, rows - tile:], right_stats_ref[0][:, :tile])
    halos = (left_ref, right_ref)
    edge_dk, edge_dv = [], []
    for i in range(2):
        q_edge = halos[i][2, 0]
        g_edge = halos[i][3, 0]
        stats = edge_stats[i]
        part = dot(edge_k[i], q_edge, NT) * factor + (edge_ref[head, i] - stats[0:1])
        prob = jnp.exp(part)
        grad = prob * (dot(edge_v[i], g_edge, NT) - stats[1:2]) * factor
        edge_dk.append(dot(grad.astype(jnp.bfloat16), q_edge, NN))
        edge_dv.append(dot(prob.astype(jnp.bfloat16), g_edge, NN))
    for ref, whole, edge in ((dk_ref, dk, edge_dk), (dv_ref, dv, edge_dv)):
        ref[0, :tile] = (whole[:tile] + edge[0]).astype(jnp.bfloat16)
        if rows > 2 * tile:
            ref[0, tile:rows - tile] = whole[tile:rows - tile].astype(jnp.bfloat16)
        ref[0, rows - tile:] = (whole[rows - tile:] + edge[1]).astype(jnp.bfloat16)


def tile_masks(tile_radius, sel_tiles, sel_count):
    band_rows, band_cols, picks = sel_tiles.shape
    tile_total = band_rows * band_cols
    tile_index = jnp.arange(tile_total, dtype=jnp.int32)
    row_of = tile_index // band_cols
    col_of = tile_index % band_cols
    spread = jnp.abs(row_of[:, None] - row_of[None, :]) + jnp.abs(col_of[:, None] - col_of[None, :])
    nearby = spread[None] <= tile_radius[:, None, None]
    live_pick = jnp.arange(picks, dtype=jnp.int32)[None, :] < sel_count.reshape(tile_total, 1)
    matches = (sel_tiles.reshape(tile_total, picks, 1) == tile_index[None, None, :]) & live_pick[
        :, :, None
    ]
    return nearby | jnp.any(matches, axis=1)[None]


def neighbours(first, last, axis):
    size = lax.axis_size(axis)
    up = [(i, i + 1) for i in range(size - 1)]
    down = [(i + 1, i) for i in range(size - 1)]
    return lax.ppermute(last, axis, up), lax.ppermute(first, axis, down)


def band_units(own, axis, work, state, later):
    size = lax.axis_size(axis)
    index = lax.axis_index(axis)
    pairs = size // 2
    side = index % 2
    swap = [(i, i ^ 1) for i in range(size)]
    step = [(i, (i + (2 if i % 2 == 0 else -2)) % size) for i in range(size)]

    def handed(x):
        return lax.ppermute(x, axis, swap)

    def passed(x):
        return lax.ppermute(x, axis, step)

    held = jnp.stack((own, handed(own)))
    units, order = [held], [index, index ^ 1]
    for s in range(1, pairs // 2 + 1):
        if s > 1:
            for fill in work[s - 2:s - 1]:
                state = fill(state)
            held, state = lax.optimization_barrier((held, state))
        if s == 2:
            held, later = lax.optimization_barrier((held, later))
        near = (index // 2 - (1 - 2 * side) * s) % pairs
        far = (index // 2 + (1 - 2 * side) * s) % pairs
        sides = [side, 1 - side]
        if 2 * s == pairs:
            held, sides = held[:1], sides[:1]
        held = passed(held)
        units += [held, handed(held)]
        order += [2 * near + i for i in sides] + [2 * far + 1 - i for i in sides]
    return units, jnp.stack(order).astype(jnp.int32), state, later


def row_bias(allowed, tile):
    bias = jnp.where(allowed, 0.0, CLOSED).astype(jnp.float32)
    heads, own, others = bias.shape
    wide = jnp.broadcast_to(bias[..., None], (heads, own, others, tile))
    return wide.reshape(heads, own, others * tile)


def on_device(query_rows, key_rows, value_rows, grad_out, sel_tiles, sel_count, tile_radius):
    heads, tile_rows, tile_cols, tile, dim = query_rows.shape
    dev_tiles = tile_rows * tile_cols
    rows = dev_tiles * tile
    factor = dim ** (-0.5)
    hb_index = lax.axis_index("hb")
    wb_index = lax.axis_index("wb")
    bands = lax.axis_size("hb")
    flat = (heads, rows, dim)
    q, k, v, g = (x.reshape(flat) for x in (query_rows, key_rows, value_rows, grad_out))
    asking = jnp.stack((q, g))
    keyed = jnp.stack((k, v))
    four = (k, v, q, g)
    left, right = neighbours(
        jnp.stack([x[:, :tile] for x in four]), jnp.stack([x[:, rows - tile:] for x in four]), "wb"
    )

    start = hb_index * dev_tiles

    def masks(state):
        reach = tile_radius >= 1
        edge_open = jnp.stack(
            (reach & (wb_index >= 1), reach & (wb_index < lax.axis_size("wb") - 1)), axis=1
        )
        edge_bias = jnp.where(edge_open, 0.0, CLOSED).astype(jnp.float32)
        return {"allowed": tile_masks(tile_radius, sel_tiles, sel_count), "edge": edge_bias}

    def own_rows(state):
        own = lax.dynamic_slice_in_dim(state["allowed"], start, dev_tiles, 1)
        return state | {"own": row_bias(own, tile)}

    def own_cols(state):
        own = lax.dynamic_slice_in_dim(state["allowed"], start, dev_tiles, 2)
        return {
            "edge": state["edge"], "own": state["own"],
            "col": row_bias(jnp.swapaxes(own, 1, 2), tile),
        }

    units, order, state, late_asking = band_units(
        keyed, "hb", (masks, own_rows, own_cols), {}, asking
    )
    own_bias, col_bias, edge_bias = state["own"], state["col"], state["edge"]
    all_asking = lax.all_gather(late_asking, "hb")

    def per_head(shape):
        return pl.BlockSpec((1,) + shape, lambda h: (h,) + (0,) * len(shape))

    smem = pl.BlockSpec(memory_space=pltpu.SMEM)
    result = per_head((rows, dim))
    pair = pl.BlockSpec((2, 1, rows, dim), lambda h: (0, h, 0, 0))

    def units_of(count):
        return pl.BlockSpec((count, 2, 1, rows, dim), lambda h: (0, 0, h, 0, 0))

    halo = pl.BlockSpec((4, 1, tile, dim), lambda h: (0, h, 0, 0))
    bias = per_head((dev_tiles, bands * rows))
    stat = per_head((2, rows))
    half = jax.ShapeDtypeStruct(flat, jnp.bfloat16)
    dq, stats = pl.pallas_call(
        functools.partial(query_side, factor=factor, tile=tile),
        grid=(heads,),
        in_specs=[smem, smem] + [units_of(u.shape[0]) for u in units] + [pair, halo, halo, bias],
        out_specs=[result, stat],
        out_shape=[half, jax.ShapeDtypeStruct((heads, 2, rows), jnp.float32)],
        name="query_side",
    )(order, edge_bias, *units, asking, left, right, own_bias)
    left_stats, right_stats = neighbours(stats, stats, "wb")
    all_stats = lax.all_gather(stats, "hb")
    dk, dv = pl.pallas_call(
        functools.partial(key_side, factor=factor, tile=tile),
        grid=(heads,),
        in_specs=[
            smem, units_of(bands),
            pl.BlockSpec((bands, 1, 2, rows), lambda h: (0, h, 0, 0)),
            pair, halo, halo, stat, stat, bias,
        ],
        out_specs=[result, result],
        out_shape=[half, half],
        name="key_side",
    )(
        edge_bias, all_asking, all_stats, keyed, left, right, left_stats, right_stats, col_bias
    )
    return tuple(x.reshape(query_rows.shape) for x in (dq, dk, dv))


def solution(mesh):
    banded = P("hd", "hb", "wb", None, None)
    return jax.shard_map(
        on_device,
        mesh=mesh,
        in_specs=(banded,) * 4 + (P(None, "wb", None), P(None, "wb"), P("hd")),
        out_specs=(banded,) * 3,
        check_vma=False,
    )
```

```python
import functools

import jax
import jax.numpy as jnp
from jax import lax
from jax.experimental import pallas as pl
from jax.experimental.pallas import tpu as pltpu
from jax.sharding import PartitionSpec as P

CLOSED = -1e30
VMEM_BYTES = 32 * 2**20
LOG2_E = 1.4426950408889634
NT = (((1,), (1,)), ((), ()))
NN = (((1,), (0,)), ((), ()))


def dot(a, b, dims):
    return lax.dot_general(a, b, dims, preferred_element_type=jnp.float32)


def as_row(col):
    n = col.shape[0]
    return jnp.transpose(jnp.broadcast_to(col, (n, n)))[0:1]


def query_side(
    edge_ref, band_ref, q_ref, g_ref, left_ref, right_ref, bias_ref, dq_ref, stats_ref, *,
    factor, tile
):
    for h in range(q_ref.shape[0]):
        query_head(
            h, edge_ref, band_ref, q_ref, g_ref, left_ref, right_ref, bias_ref, dq_ref,
            stats_ref, factor=factor, tile=tile
        )


def query_head(
    head, edge_ref, band_ref, q_ref, g_ref, left_ref, right_ref, bias_ref, dq_ref, stats_ref, *,
    factor, tile
):
    rows, dim = q_ref.shape[1:]
    keys = band_ref[:, 0, head].reshape(-1, dim)
    values = band_ref[:, 1, head].reshape(-1, dim)
    q = q_ref[head]
    g = g_ref[head]
    shaped = (rows // tile, tile, keys.shape[0])
    scores = dot(q, keys, NT) * (factor * LOG2_E)
    scores = (scores.reshape(shaped) + bias_ref[head][:, None, :]).reshape(rows, -1)
    edge_keys = (left_ref[0, head], right_ref[0, head])
    edge_values = (left_ref[1, head], right_ref[1, head])
    edge_q = (q[:tile], q[rows - tile:])
    edge_g = (g[:tile], g[rows - tile:])
    edge_scores = [
        dot(edge_q[i], edge_keys[i], NT) * (factor * LOG2_E) + edge_ref[head, i]
        for i in range(2)
    ]
    inner = rows - 2 * tile

    def spread(parts, fill):
        mid = [jnp.full((inner, 1), fill, jnp.float32)] if inner else []
        return jnp.concatenate([parts[0]] + mid + [parts[1]], axis=0)

    def own(x, i):
        return x[:tile] if i == 0 else x[rows - tile:]

    def row_sums(x):
        return jnp.sum(x, axis=1, keepdims=True)

    edge_top = spread([jnp.max(e, axis=1, keepdims=True) for e in edge_scores], CLOSED)
    top = jnp.maximum(jnp.max(scores, axis=1, keepdims=True), edge_top)
    powers = jnp.exp2(scores - top)
    edge_powers = [jnp.exp2(edge_scores[i] - own(top, i)) for i in range(2)]
    total = row_sums(powers) + spread([row_sums(e) for e in edge_powers], 0.0)
    slopes = dot(g, values, NT)
    edge_slopes = [dot(edge_g[i], edge_values[i], NT) for i in range(2)]
    scale = 1.0 / total
    weighted = row_sums(powers * slopes) + spread(
        [row_sums(edge_powers[i] * edge_slopes[i]) for i in range(2)], 0.0
    )
    delta = weighted * scale
    grad = (powers * (slopes - delta)).astype(jnp.bfloat16)
    dq = dot(grad, keys, NN)
    edge_dq = []
    for i in range(2):
        part = edge_powers[i] * (edge_slopes[i] - own(delta, i))
        edge_dq.append(dot(part.astype(jnp.bfloat16), edge_keys[i], NN))
    last = scale * factor
    dq_ref[head, :tile] = ((dq[:tile] + edge_dq[0]) * own(last, 0)).astype(jnp.bfloat16)
    if inner:
        middle = slice(tile, rows - tile)
        dq_ref[head, middle] = (dq[middle] * last[middle]).astype(jnp.bfloat16)
    dq_ref[head, rows - tile:] = ((dq[rows - tile:] + edge_dq[1]) * own(last, 1)).astype(jnp.bfloat16)
    stats_ref[head, 0:1] = as_row(top + jnp.log2(total))
    stats_ref[head, 1:2] = as_row(delta)


def key_side(
    edge_ref, band_ref, all_stats_ref, k_ref, v_ref, left_ref, right_ref, left_stats_ref,
    right_stats_ref, bias_ref, dk_ref, dv_ref, *, factor, tile
):
    for h in range(k_ref.shape[0]):
        key_head(
            h, edge_ref, band_ref, all_stats_ref, k_ref, v_ref, left_ref, right_ref,
            left_stats_ref, right_stats_ref, bias_ref, dk_ref, dv_ref, factor=factor, tile=tile
        )


def key_head(
    head, edge_ref, band_ref, all_stats_ref, k_ref, v_ref, left_ref, right_ref,
    left_stats_ref, right_stats_ref, bias_ref, dk_ref, dv_ref, *, factor, tile
):
    rows, dim = k_ref.shape[1:]
    bands = band_ref.shape[0]
    k = k_ref[head]
    v = v_ref[head]
    queries = band_ref[:, 2, head].reshape(-1, dim)
    cotan = band_ref[:, 3, head].reshape(-1, dim)
    scores = dot(k, queries, NT)
    slopes = dot(v, cotan, NT)
    grads, probs = [], []
    tiles = rows // tile
    for r in range(bands):
        at = slice(r * rows, (r + 1) * rows)
        offset = bias_ref[head][:, at] - all_stats_ref[r, head, 0:1]
        part = (scores[:, at] * (factor * LOG2_E)).reshape(tiles, tile, rows)
        prob = jnp.exp2(part + offset[:, None, :]).reshape(rows, rows)
        probs.append(prob.astype(jnp.bfloat16))
        grads.append((prob * (slopes[:, at] - all_stats_ref[r, head, 1:2])).astype(jnp.bfloat16))
    dk = dot(jnp.concatenate(grads, axis=1), queries, NN)
    dv = dot(jnp.concatenate(probs, axis=1), cotan, NN)
    edge_k = (k[:tile], k[rows - tile:])
    edge_v = (v[:tile], v[rows - tile:])
    edge_stats = (left_stats_ref[head][:, rows - tile:], right_stats_ref[head][:, :tile])
    halos = (left_ref, right_ref)
    edge_dk, edge_dv = [], []
    for i in range(2):
        q_edge = halos[i][2, head]
        g_edge = halos[i][3, head]
        stats = edge_stats[i]
        part = dot(edge_k[i], q_edge, NT) * (factor * LOG2_E)
        prob = jnp.exp2(part + (edge_ref[head, i] - stats[0:1]))
        grad = prob * (dot(edge_v[i], g_edge, NT) - stats[1:2])
        edge_dk.append(dot(grad.astype(jnp.bfloat16), q_edge, NN))
        edge_dv.append(dot(prob.astype(jnp.bfloat16), g_edge, NN))
    for ref, whole, edge, last in ((dk_ref, dk, edge_dk, factor), (dv_ref, dv, edge_dv, 1.0)):
        ref[head, :tile] = ((whole[:tile] + edge[0]) * last).astype(jnp.bfloat16)
        if rows > 2 * tile:
            ref[head, tile:rows - tile] = (whole[tile:rows - tile] * last).astype(jnp.bfloat16)
        ref[head, rows - tile:] = ((whole[rows - tile:] + edge[1]) * last).astype(jnp.bfloat16)


def tile_masks(tile_radius, sel_tiles, sel_count):
    band_rows, band_cols, picks = sel_tiles.shape
    tile_total = band_rows * band_cols
    tile_index = jnp.arange(tile_total, dtype=jnp.int32)
    row_of = tile_index // band_cols
    col_of = tile_index % band_cols
    spread = jnp.abs(row_of[:, None] - row_of[None, :]) + jnp.abs(col_of[:, None] - col_of[None, :])
    nearby = spread[None] <= tile_radius[:, None, None]
    live_pick = jnp.arange(picks, dtype=jnp.int32)[None, :] < sel_count.reshape(tile_total, 1)
    matches = (sel_tiles.reshape(tile_total, picks, 1) == tile_index[None, None, :]) & live_pick[
        :, :, None
    ]
    return nearby | jnp.any(matches, axis=1)[None]


def neighbours(first, last, axis):
    size = lax.axis_size(axis)
    up = [(i, i + 1) for i in range(size - 1)]
    down = [(i + 1, i) for i in range(size - 1)]
    return lax.ppermute(last, axis, up), lax.ppermute(first, axis, down)


def row_bias(allowed, tile):
    bias = jnp.where(allowed, 0.0, CLOSED).astype(jnp.float32)
    heads, own, others = bias.shape
    wide = jnp.broadcast_to(bias[..., None], (heads, own, others, tile))
    return wide.reshape(heads, own, others * tile)


def on_device(query_rows, key_rows, value_rows, grad_out, sel_tiles, sel_count, tile_radius):
    heads, tile_rows, tile_cols, tile, dim = query_rows.shape
    dev_tiles = tile_rows * tile_cols
    rows = dev_tiles * tile
    factor = dim ** (-0.5)
    hb_index = lax.axis_index("hb")
    wb_index = lax.axis_index("wb")
    bands = lax.axis_size("hb")
    flat = (heads, rows, dim)
    q, k, v, g = (x.reshape(flat) for x in (query_rows, key_rows, value_rows, grad_out))
    four = (k, v, q, g)
    band = lax.all_gather(jnp.stack(four), "hb")
    left, right = neighbours(
        jnp.stack([x[:, :tile] for x in four]), jnp.stack([x[:, rows - tile:] for x in four]), "wb"
    )
    allowed = tile_masks(tile_radius, sel_tiles, sel_count)
    start = hb_index * dev_tiles
    own_bias = row_bias(lax.dynamic_slice_in_dim(allowed, start, dev_tiles, 1), tile)
    col_bias = row_bias(
        jnp.swapaxes(lax.dynamic_slice_in_dim(allowed, start, dev_tiles, 2), 1, 2), tile
    )
    reach = tile_radius >= 1
    edge_open = jnp.stack(
        (reach & (wb_index >= 1), reach & (wb_index < lax.axis_size("wb") - 1)), axis=1
    )
    edge_bias = jnp.where(edge_open, 0.0, CLOSED).astype(jnp.float32)

    smem = pl.BlockSpec(memory_space=pltpu.SMEM)
    near = pl.BlockSpec(memory_space=pltpu.VMEM)
    half = jax.ShapeDtypeStruct(flat, jnp.bfloat16)
    params = pltpu.CompilerParams(vmem_limit_bytes=VMEM_BYTES)
    dq, stats = pl.pallas_call(
        functools.partial(query_side, factor=factor, tile=tile),
        in_specs=[smem] + [near] * 6,
        out_specs=[near, near],
        out_shape=[half, jax.ShapeDtypeStruct((heads, 2, rows), jnp.float32)],
        compiler_params=params,
        name="query_side",
    )(edge_bias, band, q, g, left, right, own_bias)
    all_stats = lax.all_gather(stats, "hb")
    left_stats, right_stats = neighbours(stats, stats, "wb")
    dk, dv = pl.pallas_call(
        functools.partial(key_side, factor=factor, tile=tile),
        in_specs=[smem] + [near] * 9,
        out_specs=[near, near],
        out_shape=[half, half],
        compiler_params=params,
        name="key_side",
    )(edge_bias, band, all_stats, k, v, left, right, left_stats, right_stats, col_bias)
    return tuple(x.reshape(query_rows.shape) for x in (dq, dk, dv))


def solution(mesh):
    banded = P("hd", "hb", "wb", None, None)
    return jax.shard_map(
        on_device,
        mesh=mesh,
        in_specs=(banded,) * 4 + (P(None, "wb", None), P(None, "wb"), P("hd")),
        out_specs=(banded,) * 3,
        check_vma=False,
    )
```

```python
import functools

import jax
import jax.numpy as jnp
from jax import lax
from jax.experimental import pallas as pl
from jax.experimental.pallas import tpu as pltpu
from jax.sharding import PartitionSpec as P

CLOSED = -1e30
VMEM_BYTES = 32 * 2**20
LOG2_E = 1.4426950408889634
NT = (((1,), (1,)), ((), ()))
NN = (((1,), (0,)), ((), ()))


def dot(a, b, dims):
    return lax.dot_general(a, b, dims, preferred_element_type=jnp.float32)


def as_row(col):
    n = col.shape[0]
    return jnp.transpose(jnp.broadcast_to(col, (n, n)))[0:1]


def query_side(
    place_ref, edge_ref, band_ref, left_ref, right_ref, bias_ref, dq_ref, stats_ref, *,
    factor, tile
):
    for h in range(dq_ref.shape[0]):
        query_head(
            h, place_ref, edge_ref, band_ref, left_ref, right_ref, bias_ref, dq_ref, stats_ref,
            factor=factor, tile=tile
        )


def query_head(
    head, place_ref, edge_ref, band_ref, left_ref, right_ref, bias_ref, dq_ref, stats_ref, *,
    factor, tile
):
    rows, dim = dq_ref.shape[1:]
    keys = band_ref[:, 0, head].reshape(-1, dim)
    values = band_ref[:, 1, head].reshape(-1, dim)
    q = band_ref[place_ref[0], 2, head]
    g = band_ref[place_ref[0], 3, head]
    shaped = (rows // tile, tile, keys.shape[0])
    scores = dot(q, keys, NT) * (factor * LOG2_E)
    scores = (scores.reshape(shaped) + bias_ref[head][:, None, :]).reshape(rows, -1)
    edge_keys = (left_ref[0, head], right_ref[0, head])
    edge_values = (left_ref[1, head], right_ref[1, head])
    edge_q = (q[:tile], q[rows - tile:])
    edge_g = (g[:tile], g[rows - tile:])
    edge_scores = [
        dot(edge_q[i], edge_keys[i], NT) * (factor * LOG2_E) + edge_ref[head, i]
        for i in range(2)
    ]
    inner = rows - 2 * tile

    def spread(parts, fill):
        mid = [jnp.full((inner, 1), fill, jnp.float32)] if inner else []
        return jnp.concatenate([parts[0]] + mid + [parts[1]], axis=0)

    def own(x, i):
        return x[:tile] if i == 0 else x[rows - tile:]

    def row_sums(x):
        return jnp.sum(x, axis=1, keepdims=True)

    edge_top = spread([jnp.max(e, axis=1, keepdims=True) for e in edge_scores], CLOSED)
    top = jnp.maximum(jnp.max(scores, axis=1, keepdims=True), edge_top)
    powers = jnp.exp2(scores - top)
    edge_powers = [jnp.exp2(edge_scores[i] - own(top, i)) for i in range(2)]
    total = row_sums(powers) + spread([row_sums(e) for e in edge_powers], 0.0)
    slopes = dot(g, values, NT)
    edge_slopes = [dot(edge_g[i], edge_values[i], NT) for i in range(2)]
    scale = 1.0 / total
    weighted = row_sums(powers * slopes) + spread(
        [row_sums(edge_powers[i] * edge_slopes[i]) for i in range(2)], 0.0
    )
    delta = weighted * scale
    grad = (powers * (slopes - delta)).astype(jnp.bfloat16)
    dq = dot(grad, keys, NN)
    edge_dq = []
    for i in range(2):
        part = edge_powers[i] * (edge_slopes[i] - own(delta, i))
        edge_dq.append(dot(part.astype(jnp.bfloat16), edge_keys[i], NN))
    last = scale * factor
    dq_ref[head, :tile] = ((dq[:tile] + edge_dq[0]) * own(last, 0)).astype(jnp.bfloat16)
    if inner:
        middle = slice(tile, rows - tile)
        dq_ref[head, middle] = (dq[middle] * last[middle]).astype(jnp.bfloat16)
    dq_ref[head, rows - tile:] = ((dq[rows - tile:] + edge_dq[1]) * own(last, 1)).astype(jnp.bfloat16)
    stats_ref[head, 0:1] = as_row(top + jnp.log2(total))
    stats_ref[head, 1:2] = as_row(delta)


def key_side(
    place_ref, edge_ref, band_ref, all_stats_ref, left_ref, right_ref, left_stats_ref,
    right_stats_ref, bias_ref, dk_ref, dv_ref, *, factor, tile
):
    for h in range(dk_ref.shape[0]):
        key_head(
            h, place_ref, edge_ref, band_ref, all_stats_ref, left_ref, right_ref,
            left_stats_ref, right_stats_ref, bias_ref, dk_ref, dv_ref, factor=factor, tile=tile
        )


def key_head(
    head, place_ref, edge_ref, band_ref, all_stats_ref, left_ref, right_ref,
    left_stats_ref, right_stats_ref, bias_ref, dk_ref, dv_ref, *, factor, tile
):
    rows, dim = dk_ref.shape[1:]
    bands = band_ref.shape[0]
    k = band_ref[place_ref[0], 0, head]
    v = band_ref[place_ref[0], 1, head]
    queries = band_ref[:, 2, head].reshape(-1, dim)
    cotan = band_ref[:, 3, head].reshape(-1, dim)
    scores = dot(k, queries, NT)
    slopes = dot(v, cotan, NT)
    grads, probs = [], []
    tiles = rows // tile
    for r in range(bands):
        at = slice(r * rows, (r + 1) * rows)
        offset = bias_ref[head][:, at] - all_stats_ref[r, head, 0:1]
        part = (scores[:, at] * (factor * LOG2_E)).reshape(tiles, tile, rows)
        prob = jnp.exp2(part + offset[:, None, :]).reshape(rows, rows)
        probs.append(prob.astype(jnp.bfloat16))
        grads.append((prob * (slopes[:, at] - all_stats_ref[r, head, 1:2])).astype(jnp.bfloat16))
    dk = dot(jnp.concatenate(grads, axis=1), queries, NN)
    dv = dot(jnp.concatenate(probs, axis=1), cotan, NN)
    edge_k = (k[:tile], k[rows - tile:])
    edge_v = (v[:tile], v[rows - tile:])
    edge_stats = (left_stats_ref[head][:, rows - tile:], right_stats_ref[head][:, :tile])
    halos = (left_ref, right_ref)
    edge_dk, edge_dv = [], []
    for i in range(2):
        q_edge = halos[i][2, head]
        g_edge = halos[i][3, head]
        stats = edge_stats[i]
        part = dot(edge_k[i], q_edge, NT) * (factor * LOG2_E)
        prob = jnp.exp2(part + (edge_ref[head, i] - stats[0:1]))
        grad = prob * (dot(edge_v[i], g_edge, NT) - stats[1:2])
        edge_dk.append(dot(grad.astype(jnp.bfloat16), q_edge, NN))
        edge_dv.append(dot(prob.astype(jnp.bfloat16), g_edge, NN))
    for ref, whole, edge, last in ((dk_ref, dk, edge_dk, factor), (dv_ref, dv, edge_dv, 1.0)):
        ref[head, :tile] = ((whole[:tile] + edge[0]) * last).astype(jnp.bfloat16)
        if rows > 2 * tile:
            ref[head, tile:rows - tile] = (whole[tile:rows - tile] * last).astype(jnp.bfloat16)
        ref[head, rows - tile:] = ((whole[rows - tile:] + edge[1]) * last).astype(jnp.bfloat16)


def tile_masks(tile_radius, sel_tiles, sel_count):
    band_rows, band_cols, picks = sel_tiles.shape
    tile_total = band_rows * band_cols
    tile_index = jnp.arange(tile_total, dtype=jnp.int32)
    row_of = tile_index // band_cols
    col_of = tile_index % band_cols
    spread = jnp.abs(row_of[:, None] - row_of[None, :]) + jnp.abs(col_of[:, None] - col_of[None, :])
    nearby = spread[None] <= tile_radius[:, None, None]
    live_pick = jnp.arange(picks, dtype=jnp.int32)[None, :] < sel_count.reshape(tile_total, 1)
    matches = (sel_tiles.reshape(tile_total, picks, 1) == tile_index[None, None, :]) & live_pick[
        :, :, None
    ]
    return nearby | jnp.any(matches, axis=1)[None]


def neighbours(first, last, axis):
    size = lax.axis_size(axis)
    up = [(i, i + 1) for i in range(size - 1)]
    down = [(i + 1, i) for i in range(size - 1)]
    return lax.ppermute(last, axis, up), lax.ppermute(first, axis, down)


def row_bias(allowed, tile):
    bias = jnp.where(allowed, 0.0, CLOSED).astype(jnp.float32)
    heads, own, others = bias.shape
    wide = jnp.broadcast_to(bias[..., None], (heads, own, others, tile))
    return wide.reshape(heads, own, others * tile)


def on_device(query_rows, key_rows, value_rows, grad_out, sel_tiles, sel_count, tile_radius):
    heads, tile_rows, tile_cols, tile, dim = query_rows.shape
    dev_tiles = tile_rows * tile_cols
    rows = dev_tiles * tile
    factor = dim ** (-0.5)
    hb_index = lax.axis_index("hb")
    wb_index = lax.axis_index("wb")
    bands = lax.axis_size("hb")
    flat = (heads, rows, dim)
    q, k, v, g = (x.reshape(flat) for x in (query_rows, key_rows, value_rows, grad_out))
    four = (k, v, q, g)
    band = lax.all_gather(jnp.stack(four), "hb")
    left, right = neighbours(
        jnp.stack([x[:, :tile] for x in four]), jnp.stack([x[:, rows - tile:] for x in four]), "wb"
    )
    allowed = tile_masks(tile_radius, sel_tiles, sel_count)
    start = hb_index * dev_tiles
    own_bias = row_bias(lax.dynamic_slice_in_dim(allowed, start, dev_tiles, 1), tile)
    col_bias = row_bias(
        jnp.swapaxes(lax.dynamic_slice_in_dim(allowed, start, dev_tiles, 2), 1, 2), tile
    )
    reach = tile_radius >= 1
    edge_open = jnp.stack(
        (reach & (wb_index >= 1), reach & (wb_index < lax.axis_size("wb") - 1)), axis=1
    )
    edge_bias = jnp.where(edge_open, 0.0, CLOSED).astype(jnp.float32)

    place = hb_index.astype(jnp.int32)[None]
    smem = pl.BlockSpec(memory_space=pltpu.SMEM)
    near = pl.BlockSpec(memory_space=pltpu.VMEM)
    half = jax.ShapeDtypeStruct(flat, jnp.bfloat16)
    params = pltpu.CompilerParams(vmem_limit_bytes=VMEM_BYTES)
    dq, stats = pl.pallas_call(
        functools.partial(query_side, factor=factor, tile=tile),
        in_specs=[smem, smem] + [near] * 4,
        out_specs=[near, near],
        out_shape=[half, jax.ShapeDtypeStruct((heads, 2, rows), jnp.float32)],
        compiler_params=params,
        name="query_side",
    )(place, edge_bias, band, left, right, own_bias)
    all_stats = lax.all_gather(stats, "hb")
    left_stats, right_stats = neighbours(stats, stats, "wb")
    dk, dv = pl.pallas_call(
        functools.partial(key_side, factor=factor, tile=tile),
        in_specs=[smem, smem] + [near] * 7,
        out_specs=[near, near],
        out_shape=[half, half],
        compiler_params=params,
        name="key_side",
    )(
        place, edge_bias, band, all_stats, left, right, left_stats, right_stats, col_bias
    )
    return tuple(x.reshape(query_rows.shape) for x in (dq, dk, dv))


def solution(mesh):
    banded = P("hd", "hb", "wb", None, None)
    return jax.shard_map(
        on_device,
        mesh=mesh,
        in_specs=(banded,) * 4 + (P(None, "wb", None), P(None, "wb"), P("hd")),
        out_specs=(banded,) * 3,
        check_vma=False,
    )
```

```python
import functools

import jax
import jax.numpy as jnp
from jax import lax
from jax.experimental import pallas as pl
from jax.experimental.pallas import tpu as pltpu
from jax.sharding import PartitionSpec as P

CLOSED = -1e30
VMEM_BYTES = 47 * 2**20
LOG2_E = 1.4426950408889634
NT = (((1,), (1,)), ((), ()))
NN = (((1,), (0,)), ((), ()))


def dot(a, b, dims):
    return lax.dot_general(a, b, dims, preferred_element_type=jnp.float32)


def as_row(col):
    n = col.shape[0]
    return jnp.transpose(jnp.broadcast_to(col, (n, n)))[0:1]


def query_side(
    place_ref, edge_ref, band_ref, keys_ref, values_ref, q_ref, g_ref, left_ref, right_ref, bias_ref,
    dq_ref, stats_ref, asked_ref, sems, *, factor, tile
):
    loads = [
        pltpu.make_async_copy(band_ref.at[:, 2 + i, h], asked_ref.at[h, i], sems.at[h, i])
        for h in range(asked_ref.shape[0])
        for i in range(2)
    ]

    @pl.when(pl.program_id(0) == 0)
    def _():
        for load in loads:
            load.start()

    head = pl.program_id(0)
    rows, dim = q_ref.shape[3:]
    keys = keys_ref[:, 0, 0].reshape(-1, dim)
    values = values_ref[:, 0, 0].reshape(-1, dim)
    q = q_ref[0, 0, 0]
    g = g_ref[0, 0, 0]
    shaped = (rows // tile, tile, keys.shape[0])
    scores = dot(q, keys, NT) * (factor * LOG2_E)
    scores = (scores.reshape(shaped) + bias_ref[0][:, None, :]).reshape(rows, -1)
    edge_keys = (left_ref[0, 0], right_ref[0, 0])
    edge_values = (left_ref[1, 0], right_ref[1, 0])
    edge_q = (q[:tile], q[rows - tile:])
    edge_g = (g[:tile], g[rows - tile:])
    edge_scores = [
        dot(edge_q[i], edge_keys[i], NT) * (factor * LOG2_E) + edge_ref[head, i]
        for i in range(2)
    ]
    inner = rows - 2 * tile

    def spread(parts, fill):
        mid = [jnp.full((inner, 1), fill, jnp.float32)] if inner else []
        return jnp.concatenate([parts[0]] + mid + [parts[1]], axis=0)

    def own(x, i):
        return x[:tile] if i == 0 else x[rows - tile:]

    def row_sums(x):
        return jnp.sum(x, axis=1, keepdims=True)

    edge_top = spread([jnp.max(e, axis=1, keepdims=True) for e in edge_scores], CLOSED)
    top = jnp.maximum(jnp.max(scores, axis=1, keepdims=True), edge_top)
    powers = jnp.exp2(scores - top)
    edge_powers = [jnp.exp2(edge_scores[i] - own(top, i)) for i in range(2)]
    total = row_sums(powers) + spread([row_sums(e) for e in edge_powers], 0.0)
    slopes = dot(g, values, NT)
    edge_slopes = [dot(edge_g[i], edge_values[i], NT) for i in range(2)]
    scale = 1.0 / total
    weighted = row_sums(powers * slopes) + spread(
        [row_sums(edge_powers[i] * edge_slopes[i]) for i in range(2)], 0.0
    )
    delta = weighted * scale
    grad = (powers * (slopes - delta)).astype(jnp.bfloat16)
    dq = dot(grad, keys, NN)
    edge_dq = []
    for i in range(2):
        part = edge_powers[i] * (edge_slopes[i] - own(delta, i))
        edge_dq.append(dot(part.astype(jnp.bfloat16), edge_keys[i], NN))
    last = scale * factor
    dq_ref[0, :tile] = ((dq[:tile] + edge_dq[0]) * own(last, 0)).astype(jnp.bfloat16)
    if inner:
        middle = slice(tile, rows - tile)
        dq_ref[0, middle] = (dq[middle] * last[middle]).astype(jnp.bfloat16)
    dq_ref[0, rows - tile:] = ((dq[rows - tile:] + edge_dq[1]) * own(last, 1)).astype(jnp.bfloat16)
    stats_ref[0, 0:1] = as_row(top + jnp.log2(total))
    stats_ref[0, 1:2] = as_row(delta)

    @pl.when(head == pl.num_programs(0) - 1)
    def _():
        for load in loads:
            load.wait()


def key_side(
    edge_ref, asked_ref, all_stats_ref, k_ref, v_ref, left_ref, right_ref, left_stats_ref,
    right_stats_ref, bias_ref, dk_ref, dv_ref, *, factor, tile
):
    for h in range(k_ref.shape[0]):
        key_head(
            h, edge_ref, asked_ref, all_stats_ref, k_ref, v_ref, left_ref, right_ref,
            left_stats_ref, right_stats_ref, bias_ref, dk_ref, dv_ref, factor=factor, tile=tile
        )


def key_head(
    head, edge_ref, asked_ref, all_stats_ref, k_ref, v_ref, left_ref, right_ref,
    left_stats_ref, right_stats_ref, bias_ref, dk_ref, dv_ref, *, factor, tile
):
    rows, dim = k_ref.shape[1:]
    bands = asked_ref.shape[2]
    k = k_ref[head]
    v = v_ref[head]
    queries = asked_ref[head, 0].reshape(-1, dim)
    cotan = asked_ref[head, 1].reshape(-1, dim)
    scores = dot(k, queries, NT)
    slopes = dot(v, cotan, NT)
    grads, probs = [], []
    tiles = rows // tile
    for r in range(bands):
        at = slice(r * rows, (r + 1) * rows)
        offset = bias_ref[head][:, at] - all_stats_ref[r, head, 0:1]
        part = (scores[:, at] * (factor * LOG2_E)).reshape(tiles, tile, rows)
        prob = jnp.exp2(part + offset[:, None, :]).reshape(rows, rows)
        probs.append(prob.astype(jnp.bfloat16))
        grads.append((prob * (slopes[:, at] - all_stats_ref[r, head, 1:2])).astype(jnp.bfloat16))
    dk = dot(jnp.concatenate(grads, axis=1), queries, NN)
    dv = dot(jnp.concatenate(probs, axis=1), cotan, NN)
    edge_k = (k[:tile], k[rows - tile:])
    edge_v = (v[:tile], v[rows - tile:])
    edge_stats = (left_stats_ref[head][:, rows - tile:], right_stats_ref[head][:, :tile])
    halos = (left_ref, right_ref)
    edge_dk, edge_dv = [], []
    for i in range(2):
        q_edge = halos[i][2, head]
        g_edge = halos[i][3, head]
        stats = edge_stats[i]
        part = dot(edge_k[i], q_edge, NT) * (factor * LOG2_E)
        prob = jnp.exp2(part + (edge_ref[head, i] - stats[0:1]))
        grad = prob * (dot(edge_v[i], g_edge, NT) - stats[1:2])
        edge_dk.append(dot(grad.astype(jnp.bfloat16), q_edge, NN))
        edge_dv.append(dot(prob.astype(jnp.bfloat16), g_edge, NN))
    for ref, whole, edge, last in ((dk_ref, dk, edge_dk, factor), (dv_ref, dv, edge_dv, 1.0)):
        ref[head, :tile] = ((whole[:tile] + edge[0]) * last).astype(jnp.bfloat16)
        if rows > 2 * tile:
            ref[head, tile:rows - tile] = (whole[tile:rows - tile] * last).astype(jnp.bfloat16)
        ref[head, rows - tile:] = ((whole[rows - tile:] + edge[1]) * last).astype(jnp.bfloat16)


def tile_masks(tile_radius, sel_tiles, sel_count):
    band_rows, band_cols, picks = sel_tiles.shape
    tile_total = band_rows * band_cols
    tile_index = jnp.arange(tile_total, dtype=jnp.int32)
    row_of = tile_index // band_cols
    col_of = tile_index % band_cols
    spread = jnp.abs(row_of[:, None] - row_of[None, :]) + jnp.abs(col_of[:, None] - col_of[None, :])
    nearby = spread[None] <= tile_radius[:, None, None]
    live_pick = jnp.arange(picks, dtype=jnp.int32)[None, :] < sel_count.reshape(tile_total, 1)
    matches = (sel_tiles.reshape(tile_total, picks, 1) == tile_index[None, None, :]) & live_pick[
        :, :, None
    ]
    return nearby | jnp.any(matches, axis=1)[None]


def neighbours(first, last, axis):
    size = lax.axis_size(axis)
    up = [(i, i + 1) for i in range(size - 1)]
    down = [(i + 1, i) for i in range(size - 1)]
    return lax.ppermute(last, axis, up), lax.ppermute(first, axis, down)


def row_bias(allowed, tile):
    bias = jnp.where(allowed, 0.0, CLOSED).astype(jnp.float32)
    heads, own, others = bias.shape
    wide = jnp.broadcast_to(bias[..., None], (heads, own, others, tile))
    return wide.reshape(heads, own, others * tile)


def on_device(query_rows, key_rows, value_rows, grad_out, sel_tiles, sel_count, tile_radius):
    heads, tile_rows, tile_cols, tile, dim = query_rows.shape
    dev_tiles = tile_rows * tile_cols
    rows = dev_tiles * tile
    factor = dim ** (-0.5)
    hb_index = lax.axis_index("hb")
    wb_index = lax.axis_index("wb")
    bands = lax.axis_size("hb")
    flat = (heads, rows, dim)
    q, k, v, g = (x.reshape(flat) for x in (query_rows, key_rows, value_rows, grad_out))
    four = (k, v, q, g)
    band = lax.all_gather(jnp.stack(four), "hb")
    left, right = neighbours(
        jnp.stack([x[:, :tile] for x in four]), jnp.stack([x[:, rows - tile:] for x in four]), "wb"
    )
    allowed = tile_masks(tile_radius, sel_tiles, sel_count)
    start = hb_index * dev_tiles
    own_bias = row_bias(lax.dynamic_slice_in_dim(allowed, start, dev_tiles, 1), tile)
    col_bias = row_bias(
        jnp.swapaxes(lax.dynamic_slice_in_dim(allowed, start, dev_tiles, 2), 1, 2), tile
    )
    reach = tile_radius >= 1
    edge_open = jnp.stack(
        (reach & (wb_index >= 1), reach & (wb_index < lax.axis_size("wb") - 1)), axis=1
    )
    edge_bias = jnp.where(edge_open, 0.0, CLOSED).astype(jnp.float32)

    def per_head(shape):
        return pl.BlockSpec((1,) + shape, lambda h, *_: (h,) + (0,) * len(shape))

    smem = pl.BlockSpec(memory_space=pltpu.SMEM)
    own = per_head((rows, dim))
    halo = pl.BlockSpec((4, 1, tile, dim), lambda h, *_: (0, h, 0, 0))
    bias = per_head((dev_tiles, bands * rows))
    stat = per_head((2, rows))

    def of_band(slot):
        return pl.BlockSpec((bands, 1, 1, rows, dim), lambda h, *_: (0, slot, h, 0, 0))

    half = functools.partial(jax.ShapeDtypeStruct, dtype=jnp.bfloat16)
    def of_own(slot):
        return pl.BlockSpec((1, 1, 1, rows, dim), lambda h, at: (at[0], slot, h, 0, 0))

    place = hb_index.astype(jnp.int32)[None]
    near = pl.BlockSpec(memory_space=pltpu.VMEM)
    far = pl.BlockSpec(memory_space=pltpu.HBM)
    params = pltpu.CompilerParams(vmem_limit_bytes=VMEM_BYTES)
    dq, stats, asked = pl.pallas_call(
        functools.partial(query_side, factor=factor, tile=tile),
        grid_spec=pltpu.PrefetchScalarGridSpec(
            num_scalar_prefetch=1,
            grid=(heads,),
            in_specs=[smem, far, of_band(0), of_band(1), of_own(2), of_own(3), halo, halo, bias],
            out_specs=[own, stat, near],
            scratch_shapes=[pltpu.SemaphoreType.DMA((heads, 2))],
        ),
        out_shape=[
            half(flat), jax.ShapeDtypeStruct((heads, 2, rows), jnp.float32),
            half((heads, 2, bands, rows, dim)),
        ],
        compiler_params=params,
        name="query_side",
    )(place, edge_bias, band, band, band, band, band, left, right, own_bias)
    all_stats = lax.all_gather(stats, "hb")
    left_stats, right_stats = neighbours(stats, stats, "wb")
    dk, dv = pl.pallas_call(
        functools.partial(key_side, factor=factor, tile=tile),
        in_specs=[smem] + [near] * 9,
        out_specs=[near, near],
        out_shape=[half(flat), half(flat)],
        compiler_params=params,
        name="key_side",
    )(edge_bias, asked, all_stats, k, v, left, right, left_stats, right_stats, col_bias)
    return tuple(x.reshape(query_rows.shape) for x in (dq, dk, dv))


def solution(mesh):
    banded = P("hd", "hb", "wb", None, None)
    return jax.shard_map(
        on_device,
        mesh=mesh,
        in_specs=(banded,) * 4 + (P(None, "wb", None), P(None, "wb"), P("hd")),
        out_specs=(banded,) * 3,
        check_vma=False,
    )
```
